32 devices in a mesh: pb: 8 (over y, x, core), ka: 4 (over z).
Axes of the slice: x: 2, y: 2, z: 4, core: 2. Of those that a mesh axis runs over, the one named last changes fastest.
Arguments:
- query_states: bfloat16 [16384, 512], P(('pb', 'ka')), may hold values from -128 to 128
- out_grad: bfloat16 [16384, 512], P(('pb', 'ka')), may hold values from -192 to 192
- forward_out: bfloat16 [16384, 512], P(('pb', 'ka')), may hold values from -6 to 6
- key_states: bfloat16 [16384, 128], P(('ka', 'pb')), may hold values from -8 to 8
- value_states: bfloat16 [16384, 128], P(('ka', 'pb')), may hold values from -6 to 6
- block_mask: int32 [128, 128], P('pb', 'ka'), may hold values from 0 to 1, as said below
Outputs:
- query_grad: bfloat16 [16384, 512], P(('pb', 'ka'))
- key_grad: bfloat16 [16384, 128], P(('ka', 'pb'))
- value_grad: bfloat16 [16384, 128], P(('ka', 'pb'))
The draws below stay inside these ranges and needn't reach their ends.
Inputs may be any that keep to these rules, and one draw needn't show every extreme that they name: `block_mask`: the tiles of one index of pb and one index of ka (16 query tiles by 32 key tiles) hold at most 32 ones, exactly 32 for some such group; every diagonal tile is 1.
All inputs are finite; a program needn't handle non-finite values.
Results may differ from the reference program's by a relative error of at most 0.015.
Values may be sent and summed in bfloat16 or wider, within the bound.
A program may use at most 64 MiB of HBM per device.

```python
import math
import jax
import jax.numpy as jnp
from jax import lax

TILE = 128
HD = 128
HQ = 4
QTILES = 16
NB = 128
KTILES = 32
SEQ = 16384
MOST = 32
N_PB = 8
N_KA = 4


def shared_keys(key):
    base = jax.random.normal(jax.random.fold_in(key, 11), (SEQ, HD), jnp.float32)
    base = jnp.clip(base, -6.0, 6.0)
    return base


def draw_key_states(key, part):
    base = shared_keys(key)
    return base.astype(jnp.bfloat16)


def draw_query_states(key, part):
    noise = jax.random.normal(jax.random.fold_in(key, 21), (SEQ, HQ * HD), jnp.float32)
    noise = jnp.clip(noise, -6.0, 6.0)
    return noise.astype(jnp.bfloat16)


def draw_block_mask(key, part):
    devices = N_PB * N_KA
    pairs = QTILES * KTILES
    drawn = jax.random.randint(jax.random.fold_in(key, 31), (N_PB, N_KA), 0, MOST // 2 + 1)
    spikes = jax.random.randint(jax.random.fold_in(key, 32), (N_PB, N_KA), 0, 16) == 0
    forced = jax.random.randint(jax.random.fold_in(key, 33), (), 0, devices)
    device_index = jnp.arange(devices, dtype=jnp.int32).reshape(N_PB, N_KA)
    wanted = jnp.where(spikes | (device_index == forced), MOST, drawn)
    owner = jnp.arange(N_PB, dtype=jnp.int32)[:, None] * QTILES // KTILES == jnp.arange(N_KA, dtype=jnp.int32)[None, :]
    on_diagonal = jnp.where(owner, QTILES, 0)
    allowed = jnp.minimum(wanted, MOST - on_diagonal)
    row_tile = jnp.arange(NB, dtype=jnp.int32)[:, None]
    col_tile = jnp.arange(NB, dtype=jnp.int32)[None, :]
    diagonal = (row_tile == col_tile).astype(jnp.int32)
    local = row_tile % QTILES * KTILES + col_tile % KTILES
    scores = jax.random.randint(jax.random.fold_in(key, 34), (NB, NB), 0, 2 ** 16) * pairs + local + diagonal * 2 ** 30
    grouped = scores.reshape(N_PB, QTILES, N_KA, KTILES).transpose(0, 2, 1, 3).reshape(N_PB, N_KA, pairs)
    ranks = jnp.argsort(jnp.argsort(grouped, axis=-1, stable=True), axis=-1, stable=True)
    picked = (ranks < allowed[:, :, None]).astype(jnp.int32)
    spread_back = picked.reshape(N_PB, N_KA, QTILES, KTILES).transpose(0, 2, 1, 3).reshape(NB, NB)
    return jnp.maximum(spread_back, diagonal).astype(jnp.int32)


def level_of(stream_key, shape, cuts, least, largest):
    def one(dim, shards_of):
        steps = jax.random.uniform(jax.random.fold_in(jax.random.fold_in(stream_key, 6), dim), (shards_of,), jnp.float32, least / len(cuts), largest / len(cuts))
        return jnp.repeat(jnp.exp(steps), shape[dim] // shards_of).reshape((-1,) + (1,) * (len(shape) - dim - 1))

    factor_of = one(*cuts[0])
    for cut in cuts[1:]:
        factor_of = factor_of * one(*cut)
    return factor_of


def scatter_about(own_key, extent, width, limit, shards=(), held_as=jnp.bfloat16):
    values = jax.random.normal(own_key, extent, jnp.float32) * width
    if len(shards) > 0:
        values = level_of(own_key, extent, shards, -0.22, 0.18) * values
    return jnp.clip(values, min=-limit, max=limit).astype(held_as)


def setup_inputs(seed: int = 0) -> dict:
    streams_of = jax.random.split(jax.random.key(seed), 7)
    query_states = draw_query_states(jax.random.fold_in(streams_of[6], 71), 0)
    out_grad = scatter_about(streams_of[1], (SEQ, HQ * HD), 32.0, 192.0, ((0, 32),))
    forward_out = scatter_about(streams_of[2], (SEQ, HQ * HD), 1.0, 6.0, ((0, 32),))
    key_states = draw_key_states(jax.random.fold_in(streams_of[6], 71), 0)
    value_states = scatter_about(streams_of[4], (SEQ, HD), 1.0, 6.0, ((0, 32),))
    block_mask = draw_block_mask(jax.random.fold_in(streams_of[6], 71), 0)
    return dict(query_states=query_states, out_grad=out_grad, forward_out=forward_out, key_states=key_states, value_states=value_states, block_mask=block_mask)


def reference(query_states, out_grad, forward_out, key_states, value_states, block_mask):
    score_scale = 1.0 / math.sqrt(HD)
    row_count = TILE * HQ
    product = out_grad.astype(jnp.float32) * forward_out.astype(jnp.float32)
    delta_half = lax.optimization_barrier(jnp.sum(product.reshape(SEQ, HQ, HD), axis=2)).astype(jnp.bfloat16)
    delta_all = lax.optimization_barrier(delta_half).astype(jnp.float32).reshape(N_PB, QTILES, row_count)

    def one_row(carried, inputs):
        key_acc, value_acc = carried
        row_tile, mask_row, delta_row = inputs
        flat = mask_row.astype(jnp.int32)
        ranked = (1 - flat) * NB + jnp.arange(NB, dtype=jnp.int32)
        pair_order = jnp.argsort(ranked, stable=True).astype(jnp.int32)
        pair_count = jnp.sum(flat).astype(jnp.int32)
        block_counts = lax.optimization_barrier(jnp.sum(flat.reshape(N_KA, KTILES), axis=1)).astype(jnp.int32)
        block_ends = jnp.cumsum(block_counts).astype(jnp.int32)
        block_starts = (block_ends - block_counts).astype(jnp.int32)
        row_start = (row_tile * TILE).astype(jnp.int32)
        query_tile = lax.dynamic_slice_in_dim(query_states, row_start, TILE, 0).reshape(row_count, HD)
        grad_tile = lax.dynamic_slice_in_dim(out_grad, row_start, TILE, 0).reshape(row_count, HD)

        def scores_of(col_tile):
            col_start = (col_tile * TILE).astype(jnp.int32)
            key_tile = lax.dynamic_slice_in_dim(key_states, col_start, TILE, 0)
            scores = jnp.dot(query_tile, key_tile.T, preferred_element_type=jnp.float32) * score_scale
            return (col_start, key_tile, scores)

        def forward(slot_index, current):
            row_max, row_sum = current
            _, _, scores = scores_of(pair_order[slot_index])
            new_max = jnp.maximum(row_max, lax.optimization_barrier(jnp.max(scores, axis=1)))
            new_sum = row_sum * jnp.exp(row_max - new_max) + lax.optimization_barrier(jnp.sum(jnp.exp(scores - new_max[:, None]), axis=1))
            return (new_max, new_sum)
        start_state = (jnp.full((row_count,), -1e+30, jnp.float32), jnp.zeros((row_count,), jnp.float32))
        row_max, row_sum = lax.fori_loop(jnp.int32(0), pair_count, forward, start_state)
        log_total = row_max + jnp.log(row_sum)

        def backward(slot_index, current):
            query_acc, key_part, value_part = current
            col_start, key_tile, scores = scores_of(pair_order[slot_index])
            value_tile = lax.dynamic_slice_in_dim(value_states, col_start, TILE, 0)
            probs = jnp.exp(scores - log_total[:, None])
            probs_half = probs.astype(jnp.bfloat16)
            grad_probs = jnp.dot(grad_tile, value_tile.T, preferred_element_type=jnp.float32)
            grad_scores = (probs * (grad_probs - delta_row[:, None])).astype(jnp.bfloat16)
            query_acc = query_acc + jnp.dot(grad_scores, key_tile, preferred_element_type=jnp.float32)
            key_piece = jnp.dot(grad_scores.T, query_tile, preferred_element_type=jnp.float32)
            value_piece = jnp.dot(probs_half.T, grad_tile, preferred_element_type=jnp.float32)
            key_old = lax.dynamic_slice_in_dim(key_part, col_start, TILE, 0)
            value_old = lax.dynamic_slice_in_dim(value_part, col_start, TILE, 0)
            key_part = lax.dynamic_update_slice_in_dim(key_part, key_old + key_piece, col_start, 0)
            value_part = lax.dynamic_update_slice_in_dim(value_part, value_old + value_piece, col_start, 0)
            return (query_acc, key_part, value_part)

        def per_block(block_index, current):
            query_total, key_part, value_part = current
            empty = jnp.zeros((row_count, HD), jnp.float32)
            query_part, key_part, value_part = lax.fori_loop(block_starts[block_index], block_ends[block_index], backward, (empty, key_part, value_part))
            rounded = lax.optimization_barrier(query_part.astype(jnp.bfloat16)).astype(jnp.float32)
            return (query_total + rounded, key_part, value_part)
        query_total, key_acc, value_acc = lax.fori_loop(jnp.int32(0), jnp.int32(N_KA), per_block, (jnp.zeros((row_count, HD), jnp.float32), key_acc, value_acc))
        return ((key_acc, value_acc), query_total)

    def one_block(carried, inputs):
        key_total, value_total = carried
        block_index, mask_rows, delta_rows = inputs
        rows = (block_index * QTILES + jnp.arange(QTILES, dtype=jnp.int32)).astype(jnp.int32)
        start_carry = (jnp.zeros((SEQ, HD), jnp.float32), jnp.zeros((SEQ, HD), jnp.float32))
        (key_acc, value_acc), query_parts = lax.scan(one_row, start_carry, (rows, mask_rows, delta_rows))
        key_total = key_total + lax.optimization_barrier(key_acc.astype(jnp.bfloat16)).astype(jnp.float32)
        value_total = value_total + lax.optimization_barrier(value_acc.astype(jnp.bfloat16)).astype(jnp.float32)
        return ((key_total, value_total), query_parts)
    outer_carry = (jnp.zeros((SEQ, HD), jnp.float32), jnp.zeros((SEQ, HD), jnp.float32))
    block_ids = jnp.arange(N_PB, dtype=jnp.int32)
    (key_sum, value_sum), query_parts = lax.scan(one_block, outer_carry, (block_ids, block_mask.reshape(N_PB, QTILES, NB), delta_all))
    query_grad = (query_parts.reshape(SEQ, HQ * HD) * score_scale).astype(jnp.bfloat16)
    key_grad = (key_sum * score_scale).astype(jnp.bfloat16)
    value_grad = value_sum.astype(jnp.bfloat16)
    return (query_grad, key_grad, value_grad)
```

```python
import functools
import math

import jax
import jax.numpy as jnp
from jax import lax
from jax.experimental import pallas as pl
from jax.experimental.pallas import tpu as pltpu
from jax.sharding import PartitionSpec as P

TILE = 128
HD = 128
HQ = 4
WIDE = TILE * HQ
SCALE = 1.0 / math.sqrt(HD)


NEG_START = -1e30

VMEM = pl.BlockSpec(memory_space=pltpu.VMEM)
SMEM = pl.BlockSpec(memory_space=pltpu.SMEM)
LIMIT = 60 * 1024 * 1024


def dot_nt(left, right):
    return lax.dot_general(
        left, right, (((1,), (1,)), ((), ())), preferred_element_type=jnp.float32
    )


def dot_tn(left, right):
    return lax.dot_general(
        left, right, (((0,), (0,)), ((), ())), preferred_element_type=jnp.float32
    )


def rows_of(tile):
    return pl.ds(pl.multiple_of(tile * TILE, TILE), TILE)


def stacked(ref, tile):
    block = ref[rows_of(tile), :]
    return jnp.concatenate([block[:, h * HD : (h + 1) * HD] for h in range(HQ)], axis=0)


def stats_kernel(mask_ref, q_ref, k_ref, stat_ref, list_ref, count_ref):
    row_tiles, col_tiles = mask_ref.shape
    stat_ref[0] = jnp.full((row_tiles, WIDE), NEG_START, jnp.float32)
    stat_ref[1] = jnp.zeros((row_tiles, WIDE), jnp.float32)

    def list_row(row, count):
        for col in range(col_tiles):
            list_ref[count] = row * col_tiles + col
            count = count + mask_ref[row, col]
        return count

    count = lax.fori_loop(0, row_tiles, list_row, jnp.int32(0))
    count_ref[0] = count

    def visit(slot, carried):
        pair = list_ref[slot]
        row, col = pair // col_tiles, pair % col_tiles
        scores = dot_nt(k_ref[rows_of(col), :], stacked(q_ref, row)) * SCALE
        here = pl.ds(row, 1)
        old_max = stat_ref[0, here, :]
        new_max = jnp.maximum(old_max, jnp.max(scores, axis=0, keepdims=True))
        stat_ref[1, here, :] = stat_ref[1, here, :] * jnp.exp(old_max - new_max) + jnp.sum(
            jnp.exp(scores - new_max), axis=0, keepdims=True
        )
        stat_ref[0, here, :] = new_max
        return carried

    lax.fori_loop(0, count, visit, 0)


def grad_kernel(
    col_tiles, list_ref, count_ref, stat_ref, delta_ref, q_ref, g_ref, k_ref, v_ref,
    qout_ref, kout_ref, vout_ref, log_ref, qacc_ref, kacc_ref, vacc_ref,
):
    blocks = stat_ref.shape[0]
    top = stat_ref[0, 0]
    for j in range(1, blocks):
        top = jnp.maximum(top, stat_ref[j, 0])
    total = jnp.zeros_like(top)
    for j in range(blocks):
        total = total + stat_ref[j, 1] * jnp.exp(stat_ref[j, 0] - top)
    log_ref[...] = top + jnp.log(total)
    qacc_ref[...] = jnp.zeros_like(qacc_ref)
    kacc_ref[...] = jnp.zeros_like(kacc_ref)
    vacc_ref[...] = jnp.zeros_like(vacc_ref)

    def visit(slot, carried):
        pair = list_ref[slot]
        row, col = pair // col_tiles, pair % col_tiles
        here, down = pl.ds(row, 1), rows_of(col)
        queries, grads = stacked(q_ref, row), stacked(g_ref, row)
        keys = k_ref[down, :]
        scores = dot_nt(keys, queries) * SCALE
        probs = jnp.exp(scores - log_ref[here, :])
        grad_probs = dot_nt(v_ref[down, :], grads)
        grad_scores = (probs * (grad_probs - delta_ref[here, :])).astype(jnp.bfloat16)
        vacc_ref[down, :] += jnp.dot(
            probs.astype(jnp.bfloat16), grads, preferred_element_type=jnp.float32
        )
        kacc_ref[down, :] += jnp.dot(grad_scores, queries, preferred_element_type=jnp.float32)
        piece = dot_tn(grad_scores, keys)
        for h in range(HQ):
            lanes = slice(h * HD, (h + 1) * HD)
            qacc_ref[rows_of(row), lanes] += piece[h * TILE : (h + 1) * TILE]
        return carried

    lax.fori_loop(0, count_ref[0], visit, 0)
    qout_ref[...] = qacc_ref[...].astype(jnp.bfloat16)
    kout_ref[...] = kacc_ref[...].astype(jnp.bfloat16)
    vout_ref[...] = vacc_ref[...].astype(jnp.bfloat16)


def stats_call(mask, queries, keys):
    row_tiles, col_tiles = mask.shape
    return pl.pallas_call(
        stats_kernel,
        out_shape=(
            jax.ShapeDtypeStruct((2, row_tiles, WIDE), jnp.float32),
            jax.ShapeDtypeStruct((row_tiles * col_tiles,), jnp.int32),
            jax.ShapeDtypeStruct((1,), jnp.int32),
        ),
        in_specs=[SMEM, VMEM, VMEM],
        out_specs=(VMEM, SMEM, SMEM),
        compiler_params=pltpu.CompilerParams(vmem_limit_bytes=LIMIT),
        name="stats",
    )(mask, queries, keys)


def grad_call(mask_shape, pairs, count, stats, delta, queries, grads, keys, values):
    row_tiles, col_tiles = mask_shape
    return pl.pallas_call(
        functools.partial(grad_kernel, col_tiles),
        out_shape=(
            jax.ShapeDtypeStruct(queries.shape, jnp.bfloat16),
            jax.ShapeDtypeStruct(keys.shape, jnp.bfloat16),
            jax.ShapeDtypeStruct(values.shape, jnp.bfloat16),
        ),
        in_specs=[SMEM, SMEM] + [VMEM] * 6,
        out_specs=(VMEM, VMEM, VMEM),
        scratch_shapes=[
            pltpu.VMEM((row_tiles, WIDE), jnp.float32),
            pltpu.VMEM(queries.shape, jnp.float32),
            pltpu.VMEM(keys.shape, jnp.float32),
            pltpu.VMEM(values.shape, jnp.float32),
        ],
        compiler_params=pltpu.CompilerParams(vmem_limit_bytes=LIMIT),
        name="grads",
    )(pairs, count, stats, delta, queries, grads, keys, values)


def row_delta(grad_rows, out_rows):
    product = grad_rows.astype(jnp.float32) * out_rows.astype(jnp.float32)
    summed = jnp.sum(product.reshape(-1, TILE, HQ, HD), axis=3).astype(jnp.bfloat16)
    return summed.transpose(0, 2, 1).reshape(-1, WIDE).astype(jnp.float32)


def body(query_states, out_grad, forward_out, key_states, value_states, block_mask):
    delta = row_delta(out_grad, forward_out)
    query_block = lax.all_gather(query_states, "ka", axis=0, tiled=True)
    key_block = lax.all_gather(key_states, "pb", axis=0, tiled=True)
    grad_block = lax.all_gather(out_grad, "ka", axis=0, tiled=True)
    delta_block = lax.all_gather(delta, "ka", axis=0, tiled=True)
    value_block = lax.all_gather(value_states, "pb", axis=0, tiled=True)
    stats, pairs, count = stats_call(block_mask, query_block, key_block)
    stats = lax.all_gather(stats, "ka")
    query_part, key_part, value_part = grad_call(
        block_mask.shape, pairs, count, stats, delta_block,
        query_block, grad_block, key_block, value_block,
    )
    scatter = functools.partial(lax.psum_scatter, scatter_dimension=0, tiled=True)
    query_grad = (scatter(query_part, "ka").astype(jnp.float32) * SCALE).astype(jnp.bfloat16)
    key_grad = (scatter(key_part, "pb").astype(jnp.float32) * SCALE).astype(jnp.bfloat16)
    return (query_grad, key_grad, scatter(value_part, "pb"))


def solution(mesh):
    placed = (
        P(("pb", "ka"), None),
        P(("pb", "ka"), None),
        P(("pb", "ka"), None),
        P(("ka", "pb"), None),
        P(("ka", "pb"), None),
        P("pb", "ka"),
    )
    return jax.shard_map(
        body,
        mesh=mesh,
        in_specs=placed,
        out_specs=(P(("pb", "ka"), None), P(("ka", "pb"), None), P(("ka", "pb"), None)),
        check_vma=False,
    )
```

```python
import functools
import math

import jax
import jax.numpy as jnp
from jax import lax
from jax.experimental import pallas as pl
from jax.experimental.pallas import tpu as pltpu
from jax.sharding import PartitionSpec as P

TILE = 128
HD = 128
HQ = 4
WIDE = TILE * HQ
SCALE = 1.0 / math.sqrt(HD)


NEG_START = -1e30

VMEM = pl.BlockSpec(memory_space=pltpu.VMEM)
SMEM = pl.BlockSpec(memory_space=pltpu.SMEM)
LIMIT = 60 * 1024 * 1024


def dot_nt(left, right):
    return lax.dot_general(
        left, right, (((1,), (1,)), ((), ())), preferred_element_type=jnp.float32
    )


def dot_tn(left, right):
    return lax.dot_general(
        left, right, (((0,), (0,)), ((), ())), preferred_element_type=jnp.float32
    )


def rows_of(tile):
    return pl.ds(pl.multiple_of(tile * TILE, TILE), TILE)


def stacked(ref, tile):
    block = ref[rows_of(tile), :]
    return jnp.concatenate([block[:, h * HD : (h + 1) * HD] for h in range(HQ)], axis=0)


def stats_kernel(mask_ref, q_ref, k_ref, stat_ref, list_ref, count_ref):
    row_tiles, col_tiles = mask_ref.shape
    stat_ref[0] = jnp.full((row_tiles, WIDE), NEG_START, jnp.float32)
    stat_ref[1] = jnp.zeros((row_tiles, WIDE), jnp.float32)

    def list_row(row, count):
        for col in range(col_tiles):
            list_ref[count] = row * col_tiles + col
            count = count + mask_ref[row, col]
        return count

    count = lax.fori_loop(0, row_tiles, list_row, jnp.int32(0))
    count_ref[0] = count

    def visit(slot, carried):
        pair = list_ref[slot]
        row, col = pair // col_tiles, pair % col_tiles
        scores = dot_nt(k_ref[rows_of(col), :], stacked(q_ref, row)) * SCALE
        here = pl.ds(row, 1)
        old_max = stat_ref[0, here, :]
        new_max = jnp.maximum(old_max, jnp.max(scores, axis=0, keepdims=True))
        stat_ref[1, here, :] = stat_ref[1, here, :] * jnp.exp(old_max - new_max) + jnp.sum(
            jnp.exp(scores - new_max), axis=0, keepdims=True
        )
        stat_ref[0, here, :] = new_max
        return carried

    lax.fori_loop(0, count, visit, 0)


def grad_kernel(
    col_tiles, list_ref, count_ref, stat_ref, delta_ref, q_ref, g_ref, k_ref, v_ref,
    qout_ref, kout_ref, vout_ref, log_ref, qacc_ref, kacc_ref, vacc_ref,
):
    blocks = stat_ref.shape[0]
    top = stat_ref[0, 0]
    for j in range(1, blocks):
        top = jnp.maximum(top, stat_ref[j, 0])
    total = jnp.zeros_like(top)
    for j in range(blocks):
        total = total + stat_ref[j, 1] * jnp.exp(stat_ref[j, 0] - top)
    log_ref[...] = top + jnp.log(total)
    qacc_ref[...] = jnp.zeros_like(qacc_ref)
    kacc_ref[...] = jnp.zeros_like(kacc_ref)
    vacc_ref[...] = jnp.zeros_like(vacc_ref)

    def visit(slot, carried):
        pair = list_ref[slot]
        row, col = pair // col_tiles, pair % col_tiles
        here, down = pl.ds(row, 1), rows_of(col)
        queries, grads = stacked(q_ref, row), stacked(g_ref, row)
        keys = k_ref[down, :]
        scores = dot_nt(keys, queries) * SCALE
        probs = jnp.exp(scores - log_ref[here, :])
        grad_probs = dot_nt(v_ref[down, :], grads)
        grad_scores = (probs * (grad_probs - delta_ref[here, :])).astype(jnp.bfloat16)
        vacc_ref[down, :] += jnp.dot(
            probs.astype(jnp.bfloat16), grads, preferred_element_type=jnp.float32
        )
        kacc_ref[down, :] += jnp.dot(grad_scores, queries, preferred_element_type=jnp.float32)
        piece = dot_tn(grad_scores, keys)
        for h in range(HQ):
            lanes = slice(h * HD, (h + 1) * HD)
            qacc_ref[rows_of(row), lanes] += piece[h * TILE : (h + 1) * TILE]
        return carried

    lax.fori_loop(0, count_ref[0], visit, 0)
    qout_ref[...] = qacc_ref[...].astype(jnp.bfloat16)
    kout_ref[...] = kacc_ref[...].astype(jnp.bfloat16)
    vout_ref[...] = vacc_ref[...].astype(jnp.bfloat16)


def stats_call(mask, queries, keys):
    row_tiles, col_tiles = mask.shape
    return pl.pallas_call(
        stats_kernel,
        out_shape=(
            jax.ShapeDtypeStruct((2, row_tiles, WIDE), jnp.float32),
            jax.ShapeDtypeStruct((row_tiles * col_tiles,), jnp.int32),
            jax.ShapeDtypeStruct((1,), jnp.int32),
        ),
        in_specs=[SMEM, VMEM, VMEM],
        out_specs=(VMEM, SMEM, SMEM),
        compiler_params=pltpu.CompilerParams(vmem_limit_bytes=LIMIT),
        name="stats",
    )(mask, queries, keys)


def grad_call(mask_shape, pairs, count, stats, delta, queries, grads, keys, values):
    row_tiles, col_tiles = mask_shape
    return pl.pallas_call(
        functools.partial(grad_kernel, col_tiles),
        out_shape=(
            jax.ShapeDtypeStruct(queries.shape, jnp.bfloat16),
            jax.ShapeDtypeStruct(keys.shape, jnp.bfloat16),
            jax.ShapeDtypeStruct(values.shape, jnp.bfloat16),
        ),
        in_specs=[SMEM, SMEM] + [VMEM] * 6,
        out_specs=(VMEM, VMEM, VMEM),
        scratch_shapes=[
            pltpu.VMEM((row_tiles, WIDE), jnp.float32),
            pltpu.VMEM(queries.shape, jnp.float32),
            pltpu.VMEM(keys.shape, jnp.float32),
            pltpu.VMEM(values.shape, jnp.float32),
        ],
        compiler_params=pltpu.CompilerParams(vmem_limit_bytes=LIMIT),
        name="grads",
    )(pairs, count, stats, delta, queries, grads, keys, values)


def greet(counts):
    barrier = pltpu.get_barrier_semaphore()
    for axis, count in counts.items():
        mine = lax.axis_index(axis)
        for step in range(1, count):
            pl.semaphore_signal(
                barrier, inc=1, device_id={axis: lax.rem(mine + step, count)},
                device_id_type=pl.DeviceIdType.MESH,
            )
    pl.semaphore_wait(barrier, sum(count - 1 for count in counts.values()))


def push(source, target, send, recv, axis, peer):
    copy = pltpu.make_async_remote_copy(
        src_ref=source, dst_ref=target, send_sem=send, recv_sem=recv,
        device_id={axis: peer}, device_id_type=pl.DeviceIdType.MESH,
    )
    copy.start()
    return copy


def gather_kernel(plan, *refs):
    n = len(plan)
    sources, targets, sems = refs[:n], refs[n : 2 * n], refs[2 * n :]
    greet(dict(plan))
    copies = []
    for step in range(1, max(count for _, count in plan)):
        for i, (axis, count) in enumerate(plan):
            if step < count:
                mine = lax.axis_index(axis)
                copies.append(push(
                    sources[i], targets[i].at[mine], sems[2 * i].at[step - 1],
                    sems[2 * i + 1].at[step - 1], axis, lax.rem(mine + step, count),
                ))
    for i, (axis, _) in enumerate(plan):
        targets[i][lax.axis_index(axis)] = sources[i][...]
    for copy in copies:
        copy.wait()


def sem_pairs(plan):
    return [
        pltpu.SemaphoreType.DMA((max(count - 1, 1),)) for _, count in plan for _ in range(2)
    ]


def gather_call(collective_id, name, plan, *arrays):
    return pl.pallas_call(
        functools.partial(gather_kernel, plan),
        out_shape=tuple(
            jax.ShapeDtypeStruct((count,) + a.shape, a.dtype) for (_, count), a in zip(plan, arrays)
        ),
        in_specs=[VMEM] * len(arrays),
        out_specs=(VMEM,) * len(arrays),
        scratch_shapes=sem_pairs(plan),
        compiler_params=pltpu.CompilerParams(
            collective_id=collective_id, has_side_effects=True, vmem_limit_bytes=LIMIT
        ),
        name=name,
    )(*arrays)


def scatter_kernel(plan, scales, *refs):
    n = len(plan)
    parts, outs, landed, sems = refs[:n], refs[n : 2 * n], refs[2 * n : 3 * n], refs[3 * n :]
    greet(dict(plan))
    copies = [[] for _ in plan]
    for step in range(1, max(count for _, count in plan)):
        for i, (axis, count) in enumerate(plan):
            if step < count:
                mine = lax.axis_index(axis)
                peer = lax.rem(mine + step, count)
                copies[i].append(push(
                    parts[i].at[peer], landed[i].at[step - 1], sems[2 * i].at[step - 1],
                    sems[2 * i + 1].at[step - 1], axis, peer,
                ))
    for i in reversed(range(n)):
        axis, count = plan[i]
        for copy in copies[i]:
            copy.wait()
        total = parts[i][lax.axis_index(axis)].astype(jnp.float32)
        for step in range(count - 1):
            total = total + landed[i][step].astype(jnp.float32)
        outs[i][...] = (total * scales[i]).astype(jnp.bfloat16)


def scatter_call(collective_id, name, plan, scales, *parts):
    return pl.pallas_call(
        functools.partial(scatter_kernel, plan, scales),
        out_shape=tuple(jax.ShapeDtypeStruct(p.shape[1:], jnp.bfloat16) for p in parts),
        in_specs=[VMEM] * len(parts),
        out_specs=(VMEM,) * len(parts),
        scratch_shapes=[
            pltpu.VMEM((max(count - 1, 1),) + p.shape[1:], p.dtype)
            for (_, count), p in zip(plan, parts)
        ] + sem_pairs(plan),
        compiler_params=pltpu.CompilerParams(
            collective_id=collective_id, has_side_effects=True, vmem_limit_bytes=LIMIT
        ),
        name=name,
    )(*parts)


def row_delta(grad_rows, out_rows):
    product = grad_rows.astype(jnp.float32) * out_rows.astype(jnp.float32)
    summed = jnp.sum(product.reshape(-1, TILE, HQ, HD), axis=3).astype(jnp.bfloat16)
    return summed.transpose(0, 2, 1).reshape(-1, WIDE).astype(jnp.float32)


def body(n_pb, n_ka, query_states, out_grad, forward_out, key_states, value_states, block_mask):
    delta = row_delta(out_grad, forward_out)
    ka, pb = ("ka", n_ka), ("pb", n_pb)
    gathered = gather_call(
        0, "gather", (ka, ka, ka, pb, pb), delta, query_states, out_grad, key_states, value_states
    )
    delta_block, query_block, grad_block, key_block, value_block = (
        a.reshape(-1, a.shape[-1]) for a in gathered
    )
    stats, pairs, count = stats_call(block_mask, query_block, key_block)
    (stats,) = gather_call(1, "exchange", (ka,), stats)
    query_part, key_part, value_part = grad_call(
        block_mask.shape, pairs, count, stats, delta_block,
        query_block, grad_block, key_block, value_block,
    )
    return scatter_call(
        2, "scatter", (ka, pb, pb), (SCALE, SCALE, 1.0),
        query_part.reshape((n_ka,) + query_states.shape),
        key_part.reshape((n_pb,) + key_states.shape),
        value_part.reshape((n_pb,) + value_states.shape),
    )


def solution(mesh):
    placed = (
        P(("pb", "ka"), None),
        P(("pb", "ka"), None),
        P(("pb", "ka"), None),
        P(("ka", "pb"), None),
        P(("ka", "pb"), None),
        P("pb", "ka"),
    )
    return jax.shard_map(
        functools.partial(body, mesh.shape["pb"], mesh.shape["ka"]),
        mesh=mesh,
        in_specs=placed,
        out_specs=(P(("pb", "ka"), None), P(("ka", "pb"), None), P(("ka", "pb"), None)),
        check_vma=False,
    )
```

```python
import functools
import math

import jax
import jax.numpy as jnp
from jax import lax
from jax.experimental import pallas as pl
from jax.experimental.pallas import tpu as pltpu
from jax.sharding import PartitionSpec as P

TILE = 128
HD = 128
HQ = 4
WIDE = TILE * HQ
SCALE = 1.0 / math.sqrt(HD)


NEG_START = -1e30

VMEM = pl.BlockSpec(memory_space=pltpu.VMEM)
SMEM = pl.BlockSpec(memory_space=pltpu.SMEM)
LIMIT = 60 * 1024 * 1024


def dot_nt(left, right):
    return lax.dot_general(
        left, right, (((1,), (1,)), ((), ())), preferred_element_type=jnp.float32
    )


def dot_tn(left, right):
    return lax.dot_general(
        left, right, (((0,), (0,)), ((), ())), preferred_element_type=jnp.float32
    )


def rows_of(tile):
    return pl.ds(pl.multiple_of(tile * TILE, TILE), TILE)


def stacked(ref, tile):
    block = ref[rows_of(tile), :]
    return jnp.concatenate([block[:, h * HD : (h + 1) * HD] for h in range(HQ)], axis=0)


def stats_kernel(mask_ref, q_ref, k_ref, stat_ref, list_ref, count_ref):
    row_tiles, col_tiles = mask_ref.shape
    stat_ref[0] = jnp.full((row_tiles, WIDE), NEG_START, jnp.float32)
    stat_ref[1] = jnp.zeros((row_tiles, WIDE), jnp.float32)

    def list_row(row, count):
        for col in range(col_tiles):
            list_ref[count] = row * col_tiles + col
            count = count + mask_ref[row, col]
        return count

    count = lax.fori_loop(0, row_tiles, list_row, jnp.int32(0))
    count_ref[0] = count

    def visit(slot, carried):
        pair = list_ref[slot]
        row, col = pair // col_tiles, pair % col_tiles
        scores = dot_nt(k_ref[rows_of(col), :], stacked(q_ref, row)) * SCALE
        here = pl.ds(row, 1)
        old_max = stat_ref[0, here, :]
        new_max = jnp.maximum(old_max, jnp.max(scores, axis=0, keepdims=True))
        stat_ref[1, here, :] = stat_ref[1, here, :] * jnp.exp(old_max - new_max) + jnp.sum(
            jnp.exp(scores - new_max), axis=0, keepdims=True
        )
        stat_ref[0, here, :] = new_max
        return carried

    lax.fori_loop(0, count, visit, 0)


def grad_kernel(
    col_tiles, list_ref, count_ref, stat_ref, delta_ref, q_ref, g_ref, k_ref, v_ref,
    qout_ref, kout_ref, vout_ref, log_ref, qacc_ref, kacc_ref, vacc_ref,
):
    blocks = stat_ref.shape[0]
    top = stat_ref[0, 0]
    for j in range(1, blocks):
        top = jnp.maximum(top, stat_ref[j, 0])
    total = jnp.zeros_like(top)
    for j in range(blocks):
        total = total + stat_ref[j, 1] * jnp.exp(stat_ref[j, 0] - top)
    log_ref[...] = top + jnp.log(total)
    qacc_ref[...] = jnp.zeros_like(qacc_ref)
    kacc_ref[...] = jnp.zeros_like(kacc_ref)
    vacc_ref[...] = jnp.zeros_like(vacc_ref)

    def visit(slot, carried):
        pair = list_ref[slot]
        row, col = pair // col_tiles, pair % col_tiles
        here, down = pl.ds(row, 1), rows_of(col)
        queries, grads = stacked(q_ref, row), stacked(g_ref, row)
        keys = k_ref[down, :]
        scores = dot_nt(keys, queries) * SCALE
        probs = jnp.exp(scores - log_ref[here, :])
        grad_probs = dot_nt(v_ref[down, :], grads)
        grad_scores = (probs * (grad_probs - delta_ref[here, :])).astype(jnp.bfloat16)
        vacc_ref[down, :] += jnp.dot(
            probs.astype(jnp.bfloat16), grads, preferred_element_type=jnp.float32
        )
        kacc_ref[down, :] += jnp.dot(grad_scores, queries, preferred_element_type=jnp.float32)
        piece = dot_tn(grad_scores, keys)
        for h in range(HQ):
            lanes = slice(h * HD, (h + 1) * HD)
            qacc_ref[rows_of(row), lanes] += piece[h * TILE : (h + 1) * TILE]
        return carried

    lax.fori_loop(0, count_ref[0], visit, 0)
    qout_ref[...] = qacc_ref[...].astype(jnp.bfloat16)
    kout_ref[...] = kacc_ref[...].astype(jnp.bfloat16)
    vout_ref[...] = vacc_ref[...].astype(jnp.bfloat16)


def stats_call(mask, queries, keys):
    row_tiles, col_tiles = mask.shape
    return pl.pallas_call(
        stats_kernel,
        out_shape=(
            jax.ShapeDtypeStruct((2, row_tiles, WIDE), jnp.float32),
            jax.ShapeDtypeStruct((row_tiles * col_tiles,), jnp.int32),
            jax.ShapeDtypeStruct((1,), jnp.int32),
        ),
        in_specs=[SMEM, VMEM, VMEM],
        out_specs=(VMEM, SMEM, SMEM),
        compiler_params=pltpu.CompilerParams(vmem_limit_bytes=LIMIT),
        name="stats",
    )(mask, queries, keys)


def grad_call(mask_shape, pairs, count, stats, delta, queries, grads, keys, values):
    row_tiles, col_tiles = mask_shape
    return pl.pallas_call(
        functools.partial(grad_kernel, col_tiles),
        out_shape=(
            jax.ShapeDtypeStruct(queries.shape, jnp.bfloat16),
            jax.ShapeDtypeStruct(keys.shape, jnp.bfloat16),
            jax.ShapeDtypeStruct(values.shape, jnp.bfloat16),
        ),
        in_specs=[SMEM, SMEM] + [VMEM] * 6,
        out_specs=(VMEM, VMEM, VMEM),
        scratch_shapes=[
            pltpu.VMEM((row_tiles, WIDE), jnp.float32),
            pltpu.VMEM(queries.shape, jnp.float32),
            pltpu.VMEM(keys.shape, jnp.float32),
            pltpu.VMEM(values.shape, jnp.float32),
        ],
        compiler_params=pltpu.CompilerParams(vmem_limit_bytes=LIMIT),
        name="grads",
    )(pairs, count, stats, delta, queries, grads, keys, values)


def greet(counts):
    barrier = pltpu.get_barrier_semaphore()
    for axis, count in counts.items():
        mine = lax.axis_index(axis)
        for step in range(1, count):
            pl.semaphore_signal(
                barrier, inc=1, device_id={axis: lax.rem(mine + step, count)},
                device_id_type=pl.DeviceIdType.MESH,
            )
    pl.semaphore_wait(barrier, sum(count - 1 for count in counts.values()))


def push(source, target, send, recv, axis, peer, start=True):
    copy = pltpu.make_async_remote_copy(
        src_ref=source, dst_ref=target, send_sem=send, recv_sem=recv,
        device_id={axis: peer}, device_id_type=pl.DeviceIdType.MESH,
    )
    if start:
        copy.start()
    return copy


def chain_hop(target, source, sems, which, step, forward, axis, count):
    mine = lax.axis_index(axis)
    sign = 1 if forward else -1
    sent = lax.rem(mine - sign * step + count, count)
    slot = (0 if forward else count - 1) + step
    copy = push(
        source if step == 0 else target.at[sent], target.at[sent],
        sems[2 * which].at[slot], sems[2 * which + 1].at[slot],
        axis, lax.rem(mine + sign + count, count), start=False,
    )
    if forward:
        return copy, (mine >= step) & (mine < count - 1), mine >= step + 1
    return copy, (mine + step < count) & (mine > 0), mine + step + 1 < count


def gather_kernel(plan, chained, *refs):
    n = len(plan)
    sources, targets, sems = refs[:n], refs[n : 2 * n], refs[2 * n :]
    greet(dict(plan))
    hops = {}

    def launch(step):
        for i in chained:
            axis, count = plan[i]
            for forward in (True, False):
                if step >= count - 1:
                    continue
                if step > 0:
                    before, _, lands = hops[i, step - 1, forward]
                    pl.when(lands)(before.wait_recv)
                hop = chain_hop(targets[i], sources[i], sems, i, step, forward, axis, count)
                hops[i, step, forward] = hop
                pl.when(hop[1])(hop[0].start)

    launch(0)
    copies = []
    for step in range(1, max(count for _, count in plan)):
        for i, (axis, count) in enumerate(plan):
            if step < count and i not in chained:
                mine = lax.axis_index(axis)
                copies.append(push(
                    sources[i], targets[i].at[mine], sems[2 * i].at[step - 1],
                    sems[2 * i + 1].at[step - 1], axis, lax.rem(mine + step, count),
                ))
    for i, (axis, _) in enumerate(plan):
        targets[i][lax.axis_index(axis)] = sources[i][...]
    for step in range(1, max(count for _, count in plan)):
        launch(step)
    for (i, step, forward), (copy, sends, lands) in hops.items():
        if step == plan[i][1] - 2:
            pl.when(lands)(copy.wait_recv)
        pl.when(sends)(copy.wait_send)
    for copy in copies:
        copy.wait()


def sem_pairs(plan):
    return [
        pltpu.SemaphoreType.DMA((max(2 * count - 2, 1),)) for _, count in plan for _ in range(2)
    ]


def gather_call(collective_id, name, plan, chained, *arrays):
    return pl.pallas_call(
        functools.partial(gather_kernel, plan, chained),
        out_shape=tuple(
            jax.ShapeDtypeStruct((count,) + a.shape, a.dtype) for (_, count), a in zip(plan, arrays)
        ),
        in_specs=[VMEM] * len(arrays),
        out_specs=(VMEM,) * len(arrays),
        scratch_shapes=sem_pairs(plan),
        compiler_params=pltpu.CompilerParams(
            collective_id=collective_id, has_side_effects=True, vmem_limit_bytes=LIMIT
        ),
        name=name,
    )(*arrays)


def scatter_kernel(plan, scales, *refs):
    n = len(plan)
    parts, outs, landed, sems = refs[:n], refs[n : 2 * n], refs[2 * n : 3 * n], refs[3 * n :]
    greet(dict(plan))
    copies = [[] for _ in plan]
    for step in range(1, max(count for _, count in plan)):
        for i, (axis, count) in enumerate(plan):
            if step < count:
                mine = lax.axis_index(axis)
                peer = lax.rem(mine + step, count)
                copies[i].append(push(
                    parts[i].at[peer], landed[i].at[step - 1], sems[2 * i].at[step - 1],
                    sems[2 * i + 1].at[step - 1], axis, peer,
                ))
    for i in reversed(range(n)):
        axis, count = plan[i]
        for copy in copies[i]:
            copy.wait()
        total = parts[i][lax.axis_index(axis)].astype(jnp.float32)
        for step in range(count - 1):
            total = total + landed[i][step].astype(jnp.float32)
        outs[i][...] = (total * scales[i]).astype(jnp.bfloat16)


def scatter_call(collective_id, name, plan, scales, *parts):
    return pl.pallas_call(
        functools.partial(scatter_kernel, plan, scales),
        out_shape=tuple(jax.ShapeDtypeStruct(p.shape[1:], jnp.bfloat16) for p in parts),
        in_specs=[VMEM] * len(parts),
        out_specs=(VMEM,) * len(parts),
        scratch_shapes=[
            pltpu.VMEM((max(count - 1, 1),) + p.shape[1:], p.dtype)
            for (_, count), p in zip(plan, parts)
        ] + sem_pairs(plan),
        compiler_params=pltpu.CompilerParams(
            collective_id=collective_id, has_side_effects=True, vmem_limit_bytes=LIMIT
        ),
        name=name,
    )(*parts)


def row_delta(grad_rows, out_rows):
    product = grad_rows.astype(jnp.float32) * out_rows.astype(jnp.float32)
    summed = jnp.sum(product.reshape(-1, TILE, HQ, HD), axis=3).astype(jnp.bfloat16)
    return summed.transpose(0, 2, 1).reshape(-1, WIDE).astype(jnp.float32)


def body(n_pb, n_ka, query_states, out_grad, forward_out, key_states, value_states, block_mask):
    delta = row_delta(out_grad, forward_out)
    ka, pb = ("ka", n_ka), ("pb", n_pb)
    gathered = gather_call(
        0, "gather", (ka, ka, ka, pb, pb), (1, 2), delta, query_states, out_grad, key_states, value_states
    )
    delta_block, query_block, grad_block, key_block, value_block = (
        a.reshape(-1, a.shape[-1]) for a in gathered
    )
    stats, pairs, count = stats_call(block_mask, query_block, key_block)
    (stats,) = gather_call(1, "exchange", (ka,), (), stats)
    query_part, key_part, value_part = grad_call(
        block_mask.shape, pairs, count, stats, delta_block,
        query_block, grad_block, key_block, value_block,
    )
    return scatter_call(
        2, "scatter", (ka, pb, pb), (SCALE, SCALE, 1.0),
        query_part.reshape((n_ka,) + query_states.shape),
        key_part.reshape((n_pb,) + key_states.shape),
        value_part.reshape((n_pb,) + value_states.shape),
    )


def solution(mesh):
    placed = (
        P(("pb", "ka"), None),
        P(("pb", "ka"), None),
        P(("pb", "ka"), None),
        P(("ka", "pb"), None),
        P(("ka", "pb"), None),
        P("pb", "ka"),
    )
    return jax.shard_map(
        functools.partial(body, mesh.shape["pb"], mesh.shape["ka"]),
        mesh=mesh,
        in_specs=placed,
        out_specs=(P(("pb", "ka"), None), P(("ka", "pb"), None), P(("ka", "pb"), None)),
        check_vma=False,
    )
```
